32 devices in a mesh: site: 4 (over y, x), bond: 8 (over z, core).
Axes of the slice: x: 2, y: 2, z: 4, core: 2. Of those that a mesh axis runs over, the one named last changes fastest.
Arguments:
- start_rows: bfloat16 [1024, 4096], P(None, 'bond'), may hold values from -6 to 6
- site_tensors: bfloat16 [4, 4096, 8, 4096], P('site', None, None, 'bond'), may hold values from -0.09375 to 0.09375
- block_scales: float32 [4, 8, 32], P('site', None, 'bond'), may hold values from 0.25 to 1
- displacement: float32 [4, 8, 8], P('site'), may hold values from -0.9 to 0.9
- outcomes: int32 [4, 1024], P('site'), may hold values from 0 to 7
Outputs:
- leaving: bfloat16 [4, 1024, 4096], P('site', None, 'bond')
- log_norms: float32 [4, 1024], P('site')
The draws below stay inside these ranges and needn't reach their ends.
Inputs may be any that keep to these rules, and one draw needn't show every extreme that they name: outcomes index the second dimension of displacement.
All inputs are finite; a program needn't handle non-finite values.
Results may differ from the reference program's by a relative error of at most 0.014.
Values may be sent and summed in bfloat16 or wider, within the bound.
A program may use at most 128 MiB of HBM per device.

```python
import math
import jax
import jax.numpy as jnp
from jax import lax

CHI = 4096
PHYS = 8
BLOCK = 128
SITES = 4
ALLROWS = 1024


def touch_ends(values, own_key, low, high):
    longest = values.shape.index(max(values.shape))
    spots = []
    for shift in (0, 1):
        where = [jax.random.randint(jax.random.fold_in(own_key, axis), (), 0, length) for axis, length in enumerate(values.shape)]
        where[longest] = (where[longest] + shift) % values.shape[longest]
        spots.append(tuple(where))
    return values.at[spots[0]].set(low).at[spots[1]].set(high)


def block_scale(own_key, dims, shards, least, high):
    def one(axis_at, blocks):
        steps = jax.random.uniform(jax.random.fold_in(jax.random.fold_in(own_key, 6), axis_at), (blocks,), jnp.float32, least / len(shards), high / len(shards))
        return jnp.repeat(jnp.exp(steps), dims[axis_at] // blocks).reshape((-1,) + (1,) * (len(dims) - axis_at - 1))

    loudness = one(*shards[0])
    for cut in shards[1:]:
        loudness = loudness * one(*cut)
    return loudness


def gaussian(stream_key, dims, width, most, split=(), held_as=jnp.bfloat16):
    factor_of = block_scale(stream_key, dims, split, -0.22, 0.18) if split else 1.0
    drawn = jax.random.normal(stream_key, dims, jnp.float32) * width * factor_of
    return jnp.minimum(jnp.maximum(drawn, -most), most).astype(held_as)


def setup_inputs(seed: int = 0) -> dict:
    key_of = jax.random.split(jax.random.key(seed), 6)
    return {
        "start_rows": gaussian(key_of[0], (ALLROWS, CHI), 1.0, 6.0, ((1, 8),)),
        "site_tensors": gaussian(key_of[1], (SITES, CHI, PHYS, CHI), CHI ** -0.5, 0.09375, ((0, 4), (3, 8))),
        "block_scales": jnp.clip(jnp.exp(math.log(1.0) - 1.3862944 * jax.random.uniform(key_of[2], (SITES, PHYS, CHI // BLOCK), jnp.float32) ** block_scale(key_of[2], (SITES, PHYS, CHI // BLOCK), ((0, 4), (2, 8)), -0.2, 0.2)), 0.25, 1.0),
        "displacement": gaussian(key_of[3], (SITES, PHYS, PHYS), 0.3, 0.9, ((0, 4),), jnp.float32),
        "outcomes": touch_ends(jax.random.randint(key_of[4], (SITES, ALLROWS), 0, PHYS), jax.random.fold_in(key_of[4], 1), 0, PHYS - 1).astype(jnp.int32),
    }


def reference(start_rows, site_tensors, block_scales, displacement, outcomes):
    entering = start_rows
    leaves = []
    logs = []
    for k in range(SITES):
        xf = entering.astype(jnp.float32)
        norm = jnp.sqrt(lax.optimization_barrier(jnp.mean(xf * xf, axis=1)) + 1e-06)
        logs.append(jnp.log(norm))
        prod = jnp.dot(entering, site_tensors[k].reshape(CHI, PHYS * CHI), preferred_element_type=jnp.float32)
        prod = prod.reshape(ALLROWS, PHYS, CHI // BLOCK, BLOCK) * block_scales[k][None, :, :, None]
        prod = prod.reshape(ALLROWS, PHYS, CHI)
        weight = displacement[k][outcomes[k]]
        mixed = jnp.einsum('bp,bpr->br', weight, prod)
        leave = (mixed / norm[:, None]).astype(jnp.bfloat16)
        leaves.append(leave)
        entering = leave
    return (jnp.stack(leaves), jnp.stack(logs))
```

```python
import functools
import jax
import jax.numpy as jnp
from jax import lax
from jax.experimental import pallas as pl
from jax.experimental.pallas import tpu as pltpu
from jax.sharding import PartitionSpec as P

ROWS = 128
PIECES = 2
CHUNK = 64
SLOTS = 8
LANES = 128
MESH = pl.DeviceIdType.MESH


def kernel(sites, bond, start_hbm, tensor_hbm, scale_ref, disp_ref, outcome_ref, leave_ref, log_ref,
           mats, gathered, landing, wide, total, squares, weight_ref, scales,
           start_sem, load_sem, send_up, send_down, send_pair, send_site,
           recv_line, recv_pair, recv_site):
    chi, phys, cols = tensor_hbm.shape
    allrows = leave_ref.shape[0]
    rows = min(ROWS, allrows)
    piece = rows // PIECES
    batches = allrows // rows
    chips = bond // 2
    wide_cols = 2 * cols
    chunk = min(CHUNK, wide_cols)
    site = lax.axis_index("site")
    me = lax.axis_index("bond")
    chip = me // 2
    core = me % 2
    pair = me + 1 - 2 * core
    has_up = chip < chips - 1
    has_down = chip > 0
    at_end = jnp.logical_or(chip == 0, chip == chips - 1)
    first_site = site == 0
    later_site = site > 0
    has_next = site < sites - 1

    low_half = chip < chips - 1 - chip
    spread_of = jnp.minimum(chip, chips - 1 - chip)

    def source_of(j):
        if j == 0:
            return chip
        near = chip - (j + 1) // 2 if j % 2 else chip + j // 2
        far = jnp.where(low_half, j, chips - 1 - j)
        return jnp.where(j <= 2 * spread_of, near, far)

    def block(q, source, lane_core):
        return gathered.at[source, pl.ds(pl.multiple_of(q * piece, piece), piece),
                           pl.ds(pl.multiple_of(lane_core * cols, cols), cols)]

    def line_copy(q, source, sem, to):
        ref = block(q, source, core)
        return pltpu.make_async_remote_copy(
            ref, ref, sem.at[q, source], recv_line.at[q, source],
            device_id={"bond": to}, device_id_type=MESH)

    def up_copy(q, source):
        return line_copy(q, source, send_up, me + 2)

    def down_copy(q, source):
        return line_copy(q, source, send_down, me - 2)

    def pair_copy(q, source, lane_core):
        ref = block(q, source, lane_core)
        return pltpu.make_async_remote_copy(
            ref, ref, send_pair.at[q, source], recv_pair.at[q, source],
            device_id={"bond": pair}, device_id_type=MESH)

    def site_copy(q):
        return pltpu.make_async_remote_copy(
            leave_ref.at[pl.ds(pl.multiple_of(q * piece, piece), piece), :],
            block(q, chip, core), send_site.at[q], recv_site.at[q],
            device_id={"site": site + 1}, device_id_type=MESH)

    def own(q):
        @pl.when(later_site)
        def _():
            ref = block(q, chip, core)
            pltpu.make_async_remote_copy(
                ref, ref, send_site.at[q], recv_site.at[q],
                device_id={"bond": pair}, device_id_type=MESH).wait_recv()

        @pl.when(has_down)
        def _():
            down_copy(q, chip).start()

        @pl.when(has_up)
        def _():
            up_copy(q, chip).start()

        pair_copy(q, chip, core).start()

    def arrive(q, hop):
        @pl.when(chip - hop >= 0)
        def _():
            line_copy(q, chip - hop, send_up, pair).wait_recv()

            @pl.when(has_up)
            def _():
                up_copy(q, chip - hop).start()

            pair_copy(q, chip - hop, core).start()

        @pl.when(chip + hop < chips)
        def _():
            line_copy(q, chip + hop, send_down, pair).wait_recv()

            @pl.when(has_down)
            def _():
                down_copy(q, chip + hop).start()

            pair_copy(q, chip + hop, core).start()

    per_source = wide_cols // chunk

    def load(j, i, slot):
        base = source_of(j) * wide_cols + i * chunk
        return pltpu.make_async_copy(
            tensor_hbm.at[pl.ds(pl.multiple_of(base, chunk), chunk)],
            landing.at[slot], load_sem.at[slot])

    start_copy = pltpu.make_async_copy(
        start_hbm, gathered.at[chip, :, pl.ds(pl.multiple_of(core * cols, cols), cols)], start_sem)

    @pl.when(first_site)
    def _():
        start_copy.start()

    slots = min(SLOTS, per_source)
    for step in range(slots):
        load(0, step, step).start()

    barrier = pltpu.get_barrier_semaphore()

    def greet(there, device):
        @pl.when(there)
        def _():
            pl.semaphore_signal(barrier, inc=1, device_id=device, device_id_type=MESH)

    around = ((has_up, {"bond": me + 2}), (has_down, {"bond": me - 2}),
              (chip >= 0, {"bond": pair}),
              (has_next, {"site": site + 1}), (later_site, {"site": site - 1}))
    for there, device in around:
        greet(there, device)
    peers = sum(there.astype(jnp.int32) for there, _ in around)
    pl.semaphore_wait(barrier, peers)

    @pl.when(first_site)
    def _():
        start_copy.wait()
        for h in range(PIECES):
            own(h)

    nblk = scale_ref.shape[0]
    width = cols // nblk
    for p in range(phys):
        for n in range(nblk):
            scales[p:p + 1, n * width:(n + 1) * width] = jnp.full((1, width), scale_ref[n, p], jnp.float32)
    for b in range(batches):
        row = outcome_ref[0:1, b * rows:(b + 1) * rows]
        column = jnp.transpose(jnp.broadcast_to(row, (rows, rows)))[:, :phys]
        weight = jnp.zeros((rows, phys), jnp.float32)
        for o in range(phys):
            weight = jnp.where(column == o, disp_ref[o:o + 1, :], weight)
        weight_ref[b * rows:(b + 1) * rows, :] = weight

    def spread(j):
        source = source_of(j)

        def step(i, carry):
            slot = lax.rem(i, slots)
            load(j, i, slot).wait()
            for t in range(cols // LANES):
                strip = slice(t * LANES, (t + 1) * LANES)
                wide[t] = landing[slot, :, :, strip].astype(jnp.float32).reshape(chunk * phys, LANES)
                for p in range(phys):
                    mats[p, source, pl.ds(pl.multiple_of(i * chunk, chunk), chunk), strip] = (
                        wide[t, pl.ds(p, chunk, stride=phys), :].astype(jnp.bfloat16))

            @pl.when(i + slots < per_source)
            def _():
                load(j, i + slots, slot).start()

            if j + 1 < chips:
                @pl.when(i + slots >= per_source)
                def _():
                    load(j + 1, i + slots - per_source, slot).start()
            return carry

        lax.fori_loop(0, per_source, step, 0)

    @pl.when(later_site)
    def _():
        for j in range(chips):
            spread(j)
        for h in range(PIECES):
            own(h)

    half = phys // 2

    def batch(b, carry):
        here = pl.ds(pl.multiple_of(b * rows, rows), rows)
        more = b + 1 < batches
        q = b * PIECES

        def multiply(j, part):
            source = source_of(j)
            if part == 0:
                for h in range(PIECES):
                    pair_copy(q + h, source, 1 - core).wait_recv()
                x = jnp.zeros((rows, LANES), jnp.float32)
                for t in range(wide_cols // LANES):
                    v = gathered[source, here, t * LANES:(t + 1) * LANES].astype(jnp.float32)
                    x = x + v * v
                if j == 0:
                    squares[...] = x
                else:
                    squares[...] += x
            for p in range(part * half, (part + 1) * half):
                prod = jnp.dot(gathered[source, here, :], mats[p, source], preferred_element_type=jnp.float32)
                prod = prod * scales[p:p + 1, :] * weight_ref[here, p:p + 1]
                if j == 0 and p == 0:
                    total[...] = prod
                else:
                    total[...] += prod

        for j in range(chips):
            last = j == chips - 1

            @pl.when(jnp.logical_and(first_site, b == 0))
            def _():
                spread(j)

            if not last:
                arrive(q, j + 1)
            else:
                @pl.when(jnp.logical_and(more, jnp.logical_not(at_end)))
                def _():
                    own(q + PIECES)
            multiply(j, 0)
            if not last:
                for h in range(1, PIECES):
                    arrive(q + h, j + 1)
            if j == chips - 2:
                @pl.when(jnp.logical_and(more, at_end))
                def _():
                    own(q + PIECES)
            multiply(j, 1)
        norm = jnp.sqrt(jnp.sum(squares[...], axis=1, keepdims=True) / chi + 1e-06)
        inverse = 1.0 / norm
        for h in range(PIECES):
            part = slice(h * piece, (h + 1) * piece)
            leave_ref[pl.ds(pl.multiple_of((q + h) * piece, piece), piece), :] = (
                total[part] * inverse[part]).astype(jnp.bfloat16)

            @pl.when(has_next)
            def _():
                site_copy(q + h).start()

        @pl.when(more)
        def _():
            @pl.when(jnp.logical_not(at_end))
            def _():
                for h in range(1, PIECES):
                    own(q + PIECES + h)

            @pl.when(at_end)
            def _():
                for h in range(1, PIECES):
                    own(q + PIECES + h)
        logs = jnp.transpose(jnp.broadcast_to(jnp.log(norm), (rows, rows)))
        log_ref[0:1, here] = logs[0:1, :]
        return carry

    lax.fori_loop(0, batches, batch, 0)

    def drain(q, carry):
        @pl.when(has_next)
        def _():
            site_copy(q).wait_send()
        for source in range(chips):
            pair_copy(q, source, core).wait_send()

            @pl.when(jnp.logical_and(has_up, source <= chip))
            def _():
                up_copy(q, source).wait_send()

            @pl.when(jnp.logical_and(has_down, source >= chip))
            def _():
                down_copy(q, source).wait_send()
        return carry

    lax.fori_loop(0, batches * PIECES, drain, 0)


def local(start_rows, site_tensors, block_scales, displacement, outcomes):
    sites = lax.axis_size("site")
    bond = lax.axis_size("bond")
    _, chi, phys, cols = site_tensors.shape
    allrows = start_rows.shape[0]
    rows = min(ROWS, allrows)
    pieces = allrows // rows * PIECES
    chips = bond // 2
    chunk = min(CHUNK, 2 * cols)
    slots = min(SLOTS, 2 * cols // chunk)
    sems = pltpu.SemaphoreType.DMA
    vmem = pl.BlockSpec(memory_space=pltpu.VMEM)
    leave, logs = pl.pallas_call(
        functools.partial(kernel, sites, bond),
        out_shape=(jax.ShapeDtypeStruct((allrows, cols), jnp.bfloat16),
                   jax.ShapeDtypeStruct((1, allrows), jnp.float32)),
        in_specs=[pl.BlockSpec(memory_space=pl.ANY), pl.BlockSpec(memory_space=pl.ANY),
                  pl.BlockSpec(memory_space=pltpu.SMEM), vmem, vmem],
        out_specs=(vmem, vmem),
        scratch_shapes=[
            pltpu.VMEM((phys, chips, 2 * cols, cols), jnp.bfloat16),
            pltpu.VMEM((chips, allrows, 2 * cols), jnp.bfloat16),
            pltpu.VMEM((slots, chunk, phys, cols), jnp.bfloat16),
            pltpu.VMEM((cols // LANES, chunk * phys, LANES), jnp.float32),
            pltpu.VMEM((rows, cols), jnp.float32),
            pltpu.VMEM((rows, LANES), jnp.float32),
            pltpu.VMEM((allrows, phys), jnp.float32),
            pltpu.VMEM((phys, cols), jnp.float32),
            sems(()), sems((slots,)),
            sems((pieces, chips)), sems((pieces, chips)), sems((pieces, chips)), sems((pieces,)),
            sems((pieces, chips)), sems((pieces, chips)), sems((pieces,)),
        ],
        compiler_params=pltpu.CompilerParams(
            collective_id=0, has_side_effects=True, vmem_limit_bytes=64000000),
    )(start_rows, site_tensors[0], block_scales[0].T, displacement[0], outcomes)
    return leave[None], logs


def solution(mesh):
    return jax.shard_map(
        local,
        mesh=mesh,
        in_specs=(
            P(None, "bond"),
            P("site", None, None, "bond"),
            P("site", None, "bond"),
            P("site", None, None),
            P("site", None),
        ),
        out_specs=(P("site", None, "bond"), P("site", None)),
        check_vma=False,
    )
```

```python
import functools
import jax
import jax.numpy as jnp
from jax import lax
from jax.experimental import pallas as pl
from jax.experimental.pallas import tpu as pltpu
from jax.sharding import PartitionSpec as P

ROWS = 128
PIECES = 2
AHEAD_FIRST = 1
AHEAD = 1
OWN_FIRST = 1
OWN_LATER = 3
CHUNK = 64
SLOTS = 8
LANES = 128
MESH = pl.DeviceIdType.MESH


def kernel(sites, bond, start_hbm, tensor_hbm, scale_ref, disp_ref, outcome_ref, leave_ref, log_ref,
           mats, gathered, landing, wide, total, squares, weight_ref, scales,
           start_sem, load_sem, send_up, send_down, send_pair, send_site,
           recv_line, recv_pair, recv_site):
    chi, phys, cols = tensor_hbm.shape
    allrows = leave_ref.shape[0]
    rows = min(ROWS, allrows)
    piece = rows // PIECES
    batches = allrows // rows
    chips = bond // 2
    wide_cols = 2 * cols
    chunk = min(CHUNK, wide_cols)
    site = lax.axis_index("site")
    me = lax.axis_index("bond")
    chip = me // 2
    core = me % 2
    pair = me + 1 - 2 * core
    has_up = chip < chips - 1
    has_down = chip > 0
    first_site = site == 0
    later_site = site > 0
    has_next = site < sites - 1

    low_half = chip < chips - 1 - chip
    spread_of = jnp.minimum(chip, chips - 1 - chip)

    def source_of(j):
        if j == 0:
            return chip
        near = chip - (j + 1) // 2 if j % 2 else chip + j // 2
        far = jnp.where(low_half, j, chips - 1 - j)
        return jnp.where(j <= 2 * spread_of, near, far)

    def block(q, source, lane_core):
        return gathered.at[source, pl.ds(pl.multiple_of(q * piece, piece), piece),
                           pl.ds(pl.multiple_of(lane_core * cols, cols), cols)]

    def line_copy(q, source, sem, to):
        ref = block(q, source, core)
        return pltpu.make_async_remote_copy(
            ref, ref, sem.at[q, source], recv_line.at[q, source],
            device_id={"bond": to}, device_id_type=MESH)

    def up_copy(q, source):
        return line_copy(q, source, send_up, me + 2)

    def down_copy(q, source):
        return line_copy(q, source, send_down, me - 2)

    def pair_copy(q, source, lane_core):
        ref = block(q, source, lane_core)
        return pltpu.make_async_remote_copy(
            ref, ref, send_pair.at[q, source], recv_pair.at[q, source],
            device_id={"bond": pair}, device_id_type=MESH)

    def site_copy(q):
        return pltpu.make_async_remote_copy(
            leave_ref.at[pl.ds(pl.multiple_of(q * piece, piece), piece), :],
            block(q, chip, core), send_site.at[q], recv_site.at[q],
            device_id={"site": site + 1}, device_id_type=MESH)

    def own(q):
        @pl.when(later_site)
        def _():
            ref = block(q, chip, core)
            pltpu.make_async_remote_copy(
                ref, ref, send_site.at[q], recv_site.at[q],
                device_id={"bond": pair}, device_id_type=MESH).wait_recv()

        @pl.when(has_down)
        def _():
            down_copy(q, chip).start()

        @pl.when(has_up)
        def _():
            up_copy(q, chip).start()

        pair_copy(q, chip, core).start()

    def arrive(q, hop):
        @pl.when(chip - hop >= 0)
        def _():
            line_copy(q, chip - hop, send_up, pair).wait_recv()

            @pl.when(has_up)
            def _():
                up_copy(q, chip - hop).start()

            pair_copy(q, chip - hop, core).start()

        @pl.when(chip + hop < chips)
        def _():
            line_copy(q, chip + hop, send_down, pair).wait_recv()

            @pl.when(has_down)
            def _():
                down_copy(q, chip + hop).start()

            pair_copy(q, chip + hop, core).start()

    per_source = wide_cols // chunk

    def load(j, i, slot):
        base = source_of(j) * wide_cols + i * chunk
        return pltpu.make_async_copy(
            tensor_hbm.at[pl.ds(pl.multiple_of(base, chunk), chunk)],
            landing.at[slot], load_sem.at[slot])

    start_copy = pltpu.make_async_copy(
        start_hbm, gathered.at[chip, :, pl.ds(pl.multiple_of(core * cols, cols), cols)], start_sem)

    @pl.when(first_site)
    def _():
        start_copy.start()

    slots = min(SLOTS, per_source)
    for step in range(slots):
        load(0, step, step).start()

    barrier = pltpu.get_barrier_semaphore()

    def greet(there, device):
        @pl.when(there)
        def _():
            pl.semaphore_signal(barrier, inc=1, device_id=device, device_id_type=MESH)

    around = ((has_up, {"bond": me + 2}), (has_down, {"bond": me - 2}),
              (chip >= 0, {"bond": pair}),
              (has_next, {"site": site + 1}), (later_site, {"site": site - 1}))
    for there, device in around:
        greet(there, device)
    peers = sum(there.astype(jnp.int32) for there, _ in around)
    pl.semaphore_wait(barrier, peers)

    @pl.when(first_site)
    def _():
        start_copy.wait()
        for h in range(PIECES):
            own(h)

    nblk = scale_ref.shape[0]
    width = cols // nblk
    for p in range(phys):
        for n in range(nblk):
            scales[p:p + 1, n * width:(n + 1) * width] = jnp.full((1, width), scale_ref[n, p], jnp.float32)
    for b in range(batches):
        row = outcome_ref[0:1, b * rows:(b + 1) * rows]
        column = jnp.transpose(jnp.broadcast_to(row, (rows, rows)))[:, :phys]
        weight = jnp.zeros((rows, phys), jnp.float32)
        for o in range(phys):
            weight = jnp.where(column == o, disp_ref[o:o + 1, :], weight)
        weight_ref[b * rows:(b + 1) * rows, :] = weight

    def spread(j):
        source = source_of(j)

        def step(i, carry):
            slot = lax.rem(i, slots)
            load(j, i, slot).wait()
            for t in range(cols // LANES):
                strip = slice(t * LANES, (t + 1) * LANES)
                wide[t] = landing[slot, :, :, strip].astype(jnp.float32).reshape(chunk * phys, LANES)
                for p in range(phys):
                    mats[p, source, pl.ds(pl.multiple_of(i * chunk, chunk), chunk), strip] = (
                        wide[t, pl.ds(p, chunk, stride=phys), :].astype(jnp.bfloat16))

            @pl.when(i + slots < per_source)
            def _():
                load(j, i + slots, slot).start()

            if j + 1 < chips:
                @pl.when(i + slots >= per_source)
                def _():
                    load(j + 1, i + slots - per_source, slot).start()
            return carry

        lax.fori_loop(0, per_source, step, 0)

    @pl.when(later_site)
    def _():
        for j in range(chips):
            spread(j)
        for h in range(PIECES):
            own(h)

    pieces = batches * PIECES
    half = phys // 2

    def multiply(b, j, part):
        here = pl.ds(pl.multiple_of(b * rows, rows), rows)
        source = source_of(j)
        if part == 0:
            for h in range(PIECES):
                pair_copy(b * PIECES + h, source, 1 - core).wait_recv()
            x = jnp.zeros((rows, LANES), jnp.float32)
            for t in range(wide_cols // LANES):
                v = gathered[source, here, t * LANES:(t + 1) * LANES].astype(jnp.float32)
                x = x + v * v
            if j == 0:
                squares[...] = x
            else:
                squares[...] += x
        for p in range(part * half, (part + 1) * half):
            prod = jnp.dot(gathered[source, here, :], mats[p, source], preferred_element_type=jnp.float32)
            prod = prod * scales[p:p + 1, :] * weight_ref[here, p:p + 1]
            if j == 0 and p == 0:
                total[...] = prod
            else:
                total[...] += prod

    def finish(b):
        here = pl.ds(pl.multiple_of(b * rows, rows), rows)
        norm = jnp.sqrt(jnp.sum(squares[...], axis=1, keepdims=True) / chi + 1e-06)
        inverse = 1.0 / norm
        for h in range(PIECES):
            part = slice(h * piece, (h + 1) * piece)
            q = b * PIECES + h
            leave_ref[pl.ds(pl.multiple_of(q * piece, piece), piece), :] = (
                total[part] * inverse[part]).astype(jnp.bfloat16)

            @pl.when(has_next)
            def _():
                site_copy(q).start()
        logs = jnp.transpose(jnp.broadcast_to(jnp.log(norm), (rows, rows)))
        log_ref[0:1, here] = logs[0:1, :]

    def batch(b, carry):
        q = b * PIECES
        more = b + 1 < batches
        events = [(hop, h) for hop in range(1, chips) for h in range(PIECES)]

        def handle(upto):
            while events and len(events) > PIECES * (chips - 1) - upto:
                hop, h = events.pop(0)
                arrive(q + h, hop)

        def own_next(hs, here):
            @pl.when(jnp.logical_and(more, here))
            def _():
                for h in hs:
                    own(q + PIECES + h)

        for j in range(chips):
            @pl.when(jnp.logical_and(first_site, b == 0))
            def _():
                spread(j)
            for part in range(2):
                if j == chips - 1:
                    handle(PIECES * j)
                elif part == 0:
                    handle(PIECES * j + (AHEAD_FIRST if j == 0 else AHEAD))
                else:
                    handle(PIECES * j + (PIECES if j == 0 else 2 * AHEAD))
                if 2 * j + part == min(OWN_FIRST, 2 * chips - 1):
                    own_next(range(PIECES), first_site)
                if 2 * j + part == min(OWN_LATER, 2 * chips - 1):
                    own_next(range(PIECES), later_site)
                multiply(b, j, part)
        finish(b)
        return carry

    lax.fori_loop(0, batches, batch, 0)

    def drain(q, carry):
        @pl.when(has_next)
        def _():
            site_copy(q).wait_send()
        for source in range(chips):
            pair_copy(q, source, core).wait_send()

            @pl.when(jnp.logical_and(has_up, source <= chip))
            def _():
                up_copy(q, source).wait_send()

            @pl.when(jnp.logical_and(has_down, source >= chip))
            def _():
                down_copy(q, source).wait_send()
        return carry

    lax.fori_loop(0, pieces, drain, 0)


def local(start_rows, site_tensors, block_scales, displacement, outcomes):
    sites = lax.axis_size("site")
    bond = lax.axis_size("bond")
    _, chi, phys, cols = site_tensors.shape
    allrows = start_rows.shape[0]
    rows = min(ROWS, allrows)
    pieces = allrows // rows * PIECES
    chips = bond // 2
    chunk = min(CHUNK, 2 * cols)
    slots = min(SLOTS, 2 * cols // chunk)
    sems = pltpu.SemaphoreType.DMA
    vmem = pl.BlockSpec(memory_space=pltpu.VMEM)
    leave, logs = pl.pallas_call(
        functools.partial(kernel, sites, bond),
        out_shape=(jax.ShapeDtypeStruct((allrows, cols), jnp.bfloat16),
                   jax.ShapeDtypeStruct((1, allrows), jnp.float32)),
        in_specs=[pl.BlockSpec(memory_space=pl.ANY), pl.BlockSpec(memory_space=pl.ANY),
                  pl.BlockSpec(memory_space=pltpu.SMEM), vmem, vmem],
        out_specs=(vmem, vmem),
        scratch_shapes=[
            pltpu.VMEM((phys, chips, 2 * cols, cols), jnp.bfloat16),
            pltpu.VMEM((chips, allrows, 2 * cols), jnp.bfloat16),
            pltpu.VMEM((slots, chunk, phys, cols), jnp.bfloat16),
            pltpu.VMEM((cols // LANES, chunk * phys, LANES), jnp.float32),
            pltpu.VMEM((rows, cols), jnp.float32),
            pltpu.VMEM((rows, LANES), jnp.float32),
            pltpu.VMEM((allrows, phys), jnp.float32),
            pltpu.VMEM((phys, cols), jnp.float32),
            sems(()), sems((slots,)),
            sems((pieces, chips)), sems((pieces, chips)), sems((pieces, chips)), sems((pieces,)),
            sems((pieces, chips)), sems((pieces, chips)), sems((pieces,)),
        ],
        compiler_params=pltpu.CompilerParams(
            collective_id=0, has_side_effects=True, vmem_limit_bytes=64000000),
    )(start_rows, site_tensors[0], block_scales[0].T, displacement[0], outcomes)
    return leave[None], logs


def solution(mesh):
    return jax.shard_map(
        local,
        mesh=mesh,
        in_specs=(
            P(None, "bond"),
            P("site", None, None, "bond"),
            P("site", None, "bond"),
            P("site", None, None),
            P("site", None),
        ),
        out_specs=(P("site", None, "bond"), P("site", None)),
        check_vma=False,
    )
```

```python
import functools
import jax
import jax.numpy as jnp
from jax import lax
from jax.experimental import pallas as pl
from jax.experimental.pallas import tpu as pltpu
from jax.sharding import PartitionSpec as P

ROWS = 128
PIECES = 2
AHEAD_FIRST = 1
AHEAD = 1
OWN_FIRST = 1
OWN_LATER = 3
CHUNK = 64
SLOTS = 8
LANES = 128
MESH = pl.DeviceIdType.MESH


def kernel(sites, bond, start_hbm, tensor_hbm, scale_ref, disp_ref, outcome_ref, leave_ref, log_ref,
           mats, gathered, landing, wide, total, squares, weight_ref, scales,
           start_sem, load_sem, send_up, send_down, send_pair, send_site,
           recv_line, recv_pair, recv_site):
    chi, phys, cols = tensor_hbm.shape
    allrows = leave_ref.shape[0]
    rows = min(ROWS, allrows)
    piece = rows // PIECES
    batches = allrows // rows
    chips = bond // 2
    wide_cols = 2 * cols
    chunk = min(CHUNK, wide_cols)
    site = lax.axis_index("site")
    me = lax.axis_index("bond")
    chip = me // 2
    core = me % 2
    pair = me + 1 - 2 * core
    has_up = chip < chips - 1
    has_down = chip > 0
    first_site = site == 0
    at_end = jnp.logical_or(chip == 0, chip == chips - 1)
    later_site = site > 0
    has_next = site < sites - 1

    low_half = chip < chips - 1 - chip
    spread_of = jnp.minimum(chip, chips - 1 - chip)

    def source_of(j):
        if j == 0:
            return chip
        near = chip - (j + 1) // 2 if j % 2 else chip + j // 2
        far = jnp.where(low_half, j, chips - 1 - j)
        return jnp.where(j <= 2 * spread_of, near, far)

    def block(q, source, lane_core):
        return gathered.at[source, pl.ds(pl.multiple_of(q * piece, piece), piece),
                           pl.ds(pl.multiple_of(lane_core * cols, cols), cols)]

    def line_copy(q, source, sem, to):
        ref = block(q, source, core)
        return pltpu.make_async_remote_copy(
            ref, ref, sem.at[q, source], recv_line.at[q, source],
            device_id={"bond": to}, device_id_type=MESH)

    def up_copy(q, source):
        return line_copy(q, source, send_up, me + 2)

    def down_copy(q, source):
        return line_copy(q, source, send_down, me - 2)

    def pair_copy(q, source, lane_core):
        ref = block(q, source, lane_core)
        return pltpu.make_async_remote_copy(
            ref, ref, send_pair.at[q, source], recv_pair.at[q, source],
            device_id={"bond": pair}, device_id_type=MESH)

    def site_copy(q):
        return pltpu.make_async_remote_copy(
            leave_ref.at[pl.ds(pl.multiple_of(q * piece, piece), piece), :],
            block(q, chip, core), send_site.at[q], recv_site.at[q],
            device_id={"site": site + 1}, device_id_type=MESH)

    def own(q):
        @pl.when(later_site)
        def _():
            ref = block(q, chip, core)
            pltpu.make_async_remote_copy(
                ref, ref, send_site.at[q], recv_site.at[q],
                device_id={"bond": pair}, device_id_type=MESH).wait_recv()

        @pl.when(has_down)
        def _():
            down_copy(q, chip).start()

        @pl.when(has_up)
        def _():
            up_copy(q, chip).start()

        pair_copy(q, chip, core).start()

    def arrive(q, hop):
        @pl.when(chip - hop >= 0)
        def _():
            line_copy(q, chip - hop, send_up, pair).wait_recv()

            @pl.when(has_up)
            def _():
                up_copy(q, chip - hop).start()

            pair_copy(q, chip - hop, core).start()

        @pl.when(chip + hop < chips)
        def _():
            line_copy(q, chip + hop, send_down, pair).wait_recv()

            @pl.when(has_down)
            def _():
                down_copy(q, chip + hop).start()

            pair_copy(q, chip + hop, core).start()

    per_source = wide_cols // chunk

    def load(j, i, slot):
        base = source_of(j) * wide_cols + i * chunk
        return pltpu.make_async_copy(
            tensor_hbm.at[pl.ds(pl.multiple_of(base, chunk), chunk)],
            landing.at[slot], load_sem.at[slot])

    start_copy = pltpu.make_async_copy(
        start_hbm, gathered.at[chip, :, pl.ds(pl.multiple_of(core * cols, cols), cols)], start_sem)

    @pl.when(first_site)
    def _():
        start_copy.start()

    slots = min(SLOTS, per_source)
    for step in range(slots):
        load(0, step, step).start()

    barrier = pltpu.get_barrier_semaphore()

    def greet(there, device):
        @pl.when(there)
        def _():
            pl.semaphore_signal(barrier, inc=1, device_id=device, device_id_type=MESH)

    around = ((has_up, {"bond": me + 2}), (has_down, {"bond": me - 2}),
              (chip >= 0, {"bond": pair}),
              (has_next, {"site": site + 1}), (later_site, {"site": site - 1}))
    for there, device in around:
        greet(there, device)
    peers = sum(there.astype(jnp.int32) for there, _ in around)
    pl.semaphore_wait(barrier, peers)

    @pl.when(first_site)
    def _():
        start_copy.wait()
        for h in range(PIECES):
            own(h)

    nblk = scale_ref.shape[0]
    width = cols // nblk
    for p in range(phys):
        for n in range(nblk):
            scales[p:p + 1, n * width:(n + 1) * width] = jnp.full((1, width), scale_ref[n, p], jnp.float32)
    for b in range(batches):
        row = outcome_ref[0:1, b * rows:(b + 1) * rows]
        column = jnp.transpose(jnp.broadcast_to(row, (rows, rows)))[:, :phys]
        weight = jnp.zeros((rows, phys), jnp.float32)
        for o in range(phys):
            weight = jnp.where(column == o, disp_ref[o:o + 1, :], weight)
        weight_ref[b * rows:(b + 1) * rows, :] = weight

    def spread(j, first, end):
        source = source_of(j)

        def step(i, carry):
            slot = lax.rem(i, slots)
            load(j, i, slot).wait()
            for t in range(cols // LANES):
                strip = slice(t * LANES, (t + 1) * LANES)
                wide[t] = landing[slot, :, :, strip].astype(jnp.float32).reshape(chunk * phys, LANES)
                for p in range(phys):
                    mats[p, source, pl.ds(pl.multiple_of(i * chunk, chunk), chunk), strip] = (
                        wide[t, pl.ds(p, chunk, stride=phys), :].astype(jnp.bfloat16))

            @pl.when(i + slots < per_source)
            def _():
                load(j, i + slots, slot).start()

            if j + 1 < chips:
                @pl.when(i + slots >= per_source)
                def _():
                    load(j + 1, i + slots - per_source, slot).start()
            return carry

        lax.fori_loop(first, end, step, 0)

    @pl.when(later_site)
    def _():
        for j in range(chips):
            spread(j, 0, per_source)
        for h in range(PIECES):
            own(h)

    pieces = batches * PIECES
    ahead = first_site.astype(jnp.int32)

    @pl.when(first_site)
    def _():
        for j in range(chips):
            for h in range(PIECES):
                spread(j, h * per_source // PIECES, (h + 1) * per_source // PIECES)
                if j + 1 < chips:
                    arrive(h, j + 1)
                if j >= 2 and batches > 1:
                    arrive(PIECES + h, j - 1)
            if j in (0, 2) and batches > j // 2 + 1:
                for h in range(PIECES):
                    own((j // 2 + 1) * PIECES + h)
    half = phys // 2

    def multiply(b, j, part):
        here = pl.ds(pl.multiple_of(b * rows, rows), rows)
        source = source_of(j)
        if part == 0:
            for h in range(PIECES):
                pair_copy(b * PIECES + h, source, 1 - core).wait_recv()
            x = jnp.zeros((rows, LANES), jnp.float32)
            for t in range(wide_cols // LANES):
                v = gathered[source, here, t * LANES:(t + 1) * LANES].astype(jnp.float32)
                x = x + v * v
            if j == 0:
                squares[...] = x
            else:
                squares[...] += x
        for p in range(part * half, (part + 1) * half):
            prod = jnp.dot(gathered[source, here, :], mats[p, source], preferred_element_type=jnp.float32)
            prod = prod * scales[p:p + 1, :] * weight_ref[here, p:p + 1]
            if j == 0 and p == 0:
                total[...] = prod
            else:
                total[...] += prod

    def finish(b):
        here = pl.ds(pl.multiple_of(b * rows, rows), rows)
        norm = jnp.sqrt(jnp.sum(squares[...], axis=1, keepdims=True) / chi + 1e-06)
        inverse = 1.0 / norm
        for h in range(PIECES):
            part = slice(h * piece, (h + 1) * piece)
            q = b * PIECES + h
            leave_ref[pl.ds(pl.multiple_of(q * piece, piece), piece), :] = (
                total[part] * inverse[part]).astype(jnp.bfloat16)

            @pl.when(has_next)
            def _():
                site_copy(q).start()
        logs = jnp.transpose(jnp.broadcast_to(jnp.log(norm), (rows, rows)))
        log_ref[0:1, here] = logs[0:1, :]

    def batch(b, carry):
        q = b * PIECES
        events = [(hop, h) for hop in range(1, chips) for h in range(PIECES)]
        begun = jnp.logical_and(first_site, b == 0)

        def handle(upto):
            while events and len(events) > PIECES * (chips - 1) - upto:
                hop, h = events.pop(0)
                due = b + ahead < batches
                if hop <= chips - 2:
                    due = jnp.logical_and(due, jnp.logical_not(begun))

                @pl.when(due)
                def _():
                    arrive(q + ahead * PIECES + h, hop)

        def own_next(later, here):
            due = jnp.logical_and(here, b + later < batches)

            @pl.when(jnp.logical_and(due, jnp.logical_not(begun)))
            def _():
                for h in range(PIECES):
                    own(q + later * PIECES + h)

        for j in range(chips):
            for part in range(2):
                if j == chips - 1:
                    handle(PIECES * j)
                elif part == 0:
                    handle(PIECES * j + (AHEAD_FIRST if j == 0 else AHEAD))
                else:
                    handle(PIECES * j + (PIECES if j == 0 else 2 * AHEAD))
                if 2 * j + part == min(OWN_FIRST, 2 * chips - 1):
                    own_next(2, first_site)
                if 2 * j + part == 1:
                    own_next(1, jnp.logical_and(later_site, at_end))
                if 2 * j + part == 3:
                    own_next(1, jnp.logical_and(later_site, jnp.logical_not(at_end)))
                multiply(b, j, part)
        finish(b)
        return carry

    lax.fori_loop(0, batches, batch, 0)

    def drain(q, carry):
        @pl.when(has_next)
        def _():
            site_copy(q).wait_send()
        for source in range(chips):
            pair_copy(q, source, core).wait_send()

            @pl.when(jnp.logical_and(has_up, source <= chip))
            def _():
                up_copy(q, source).wait_send()

            @pl.when(jnp.logical_and(has_down, source >= chip))
            def _():
                down_copy(q, source).wait_send()
        return carry

    lax.fori_loop(0, pieces, drain, 0)


def local(start_rows, site_tensors, block_scales, displacement, outcomes):
    sites = lax.axis_size("site")
    bond = lax.axis_size("bond")
    _, chi, phys, cols = site_tensors.shape
    allrows = start_rows.shape[0]
    rows = min(ROWS, allrows)
    pieces = allrows // rows * PIECES
    chips = bond // 2
    chunk = min(CHUNK, 2 * cols)
    slots = min(SLOTS, 2 * cols // chunk)
    sems = pltpu.SemaphoreType.DMA
    vmem = pl.BlockSpec(memory_space=pltpu.VMEM)
    leave, logs = pl.pallas_call(
        functools.partial(kernel, sites, bond),
        out_shape=(jax.ShapeDtypeStruct((allrows, cols), jnp.bfloat16),
                   jax.ShapeDtypeStruct((1, allrows), jnp.float32)),
        in_specs=[pl.BlockSpec(memory_space=pl.ANY), pl.BlockSpec(memory_space=pl.ANY),
                  pl.BlockSpec(memory_space=pltpu.SMEM), vmem, vmem],
        out_specs=(vmem, vmem),
        scratch_shapes=[
            pltpu.VMEM((phys, chips, 2 * cols, cols), jnp.bfloat16),
            pltpu.VMEM((chips, allrows, 2 * cols), jnp.bfloat16),
            pltpu.VMEM((slots, chunk, phys, cols), jnp.bfloat16),
            pltpu.VMEM((cols // LANES, chunk * phys, LANES), jnp.float32),
            pltpu.VMEM((rows, cols), jnp.float32),
            pltpu.VMEM((rows, LANES), jnp.float32),
            pltpu.VMEM((allrows, phys), jnp.float32),
            pltpu.VMEM((phys, cols), jnp.float32),
            sems(()), sems((slots,)),
            sems((pieces, chips)), sems((pieces, chips)), sems((pieces, chips)), sems((pieces,)),
            sems((pieces, chips)), sems((pieces, chips)), sems((pieces,)),
        ],
        compiler_params=pltpu.CompilerParams(
            collective_id=0, has_side_effects=True, vmem_limit_bytes=64000000),
    )(start_rows, site_tensors[0], block_scales[0].T, displacement[0], outcomes)
    return leave[None], logs


def solution(mesh):
    return jax.shard_map(
        local,
        mesh=mesh,
        in_specs=(
            P(None, "bond"),
            P("site", None, None, "bond"),
            P("site", None, "bond"),
            P("site", None, None),
            P("site", None),
        ),
        out_specs=(P("site", None, "bond"), P("site", None)),
        check_vma=False,
    )
```
